512 devices in a mesh: ctx: 64 (over z, y), tp: 8 (over x, core).
Axes of the slice: x: 4, y: 8, z: 8, core: 2. Of those that a mesh axis runs over, the one named last changes fastest.
Arguments:
- query_in: bfloat16 [16384, 2048], P('ctx', 'tp'), may hold values from -6 to 6
- key_in: bfloat16 [16384, 2048], P('ctx', 'tp'), may hold values from -6 to 6
- value_in: bfloat16 [16384, 4096], P('ctx', 'tp'), may hold values from -6 to 6
- gate_values: bfloat16 [16384, 4096], P('ctx', 'tp'), may hold values from -6 to 6
- query_conv: bfloat16 [4, 2048], P(None, 'tp'), may hold values from -3 to 3
- key_conv: bfloat16 [4, 2048], P(None, 'tp'), may hold values from -3 to 3
- value_conv: bfloat16 [4, 4096], P(None, 'tp'), may hold values from -3 to 3
- beta_rate: float32 [32, 16384], P('tp', 'ctx'), may hold values from 0.002 to 0.9, as said below
- log_decay: float32 [32, 16384], P('tp', 'ctx'), may hold values from -0.8 to 0, as said below
- norm_gain: float32 [128], replicated, may hold values from 0.1 to 1.9
- out_weight: bfloat16 [4096, 2048], P('tp'), may hold values from -0.09375 to 0.09375
Outputs:
- layer_out: bfloat16 [16384, 2048], P(('ctx', 'tp'))
The draws below stay inside these ranges and needn't reach their ends.
Inputs may be any that keep to these rules, and one draw needn't show every extreme that they name: beta_rate lies strictly between 0 and 1. log_decay is never positive.
All inputs are finite; a program needn't handle non-finite values.
Results may differ from the reference program's by a relative error of at most 0.014.
Values may be sent and summed in bfloat16 or wider, within the bound.
No kernel may reach another device: no remote copies, remote signals or barrier semaphores. Data moves between devices by JAX's collectives and lax.ppermute only.
A program may use at most 128 MiB of HBM per device.

```python
import jax
import jax.numpy as jnp
from jax import lax

D = 2048
HK = 16
HV = 32
DK = 128
DV = 128
KW = 4
BLOCK = 64
TOKENS = 16384
N_TP = 8


def head_kinds(key, cutoff):
    labels = jax.random.randint(jax.random.fold_in(key, 11), (HV,), 0, 8)
    return labels < cutoff


def draw_beta_rate(key, part):
    cutoff = 4
    is_fast = head_kinds(key, cutoff)
    uniform_draw = jax.random.uniform(jax.random.fold_in(key, 21), (HV, TOKENS), jnp.float32)
    fast_rate = 0.3 + 0.6 * uniform_draw
    slow_rate = 0.002 * jnp.exp(uniform_draw * jnp.log(10.0))
    return jnp.where(is_fast[:, None], fast_rate, slow_rate).astype(jnp.float32)


def draw_log_decay(key, part):
    cutoff = 4
    is_fast = head_kinds(key, cutoff)
    jitter = jnp.exp(jax.random.uniform(jax.random.fold_in(key, 41), (HV, TOKENS), jnp.float32, -0.69, 0.69))
    block_scale = jnp.exp(jax.random.uniform(jax.random.fold_in(key, 42), (HV, 16), jnp.float32, -0.69, 0.69))
    block_scale = jnp.repeat(block_scale, TOKENS // 16, axis=1)
    base_rate = jnp.where(is_fast[:, None], 1.0 / 40.0, 0.5 / TOKENS)
    beta_strength = base_rate * jitter * block_scale
    token_positions = jax.random.randint(jax.random.fold_in(key, 43), (HV, 4, 1), 0, TOKENS)
    token_places = lax.broadcasted_iota(jnp.int32, (HV, 4, TOKENS), 2)
    token_groups_list = jnp.any(token_places == token_positions, axis=1)
    layer_depth = jax.random.uniform(jax.random.fold_in(key, 44), (HV, TOKENS), jnp.float32, 0.22, 0.69)
    return (-(beta_strength + jnp.where(token_groups_list, layer_depth, 0.0))).astype(jnp.float32)


def steps_of(stream_key, dims, pieces, least, high):
    factor_of, own = 1.0, jax.random.fold_in(stream_key, 6)
    for dim, shards_of in pieces:
        heights = jnp.exp(jax.random.uniform(jax.random.fold_in(own, dim), (shards_of,), jnp.float32, least / len(pieces), high / len(pieces)))
        factor_of = factor_of * jnp.repeat(heights, dims[dim] // shards_of).reshape([-1 if axis == dim else 1 for axis in range(len(dims))])
    return factor_of


def bell_draw(own_key, extent, scale, most, pieces=(), kind=jnp.bfloat16):
    drawn = jax.random.normal(own_key, extent, jnp.float32) * scale
    if len(pieces) > 0:
        drawn = steps_of(own_key, extent, pieces, -0.22, 0.18) * drawn
    return jnp.clip(drawn, min=-most, max=most).astype(kind)


def setup_inputs(seed: int = 0) -> dict:
    key_list = jax.random.split(jax.random.key(seed), 12)
    return {
        "query_in": bell_draw(key_list[0], (TOKENS, HK * DK), 1.0, 6.0, ((0, 64), (1, 8))),
        "key_in": bell_draw(key_list[1], (TOKENS, HK * DK), 1.0, 6.0, ((0, 64), (1, 8))),
        "value_in": bell_draw(key_list[2], (TOKENS, HV * DV), 1.0, 6.0, ((0, 64), (1, 8))),
        "gate_values": bell_draw(key_list[3], (TOKENS, HV * DV), 1.0, 6.0, ((0, 64), (1, 8))),
        "query_conv": bell_draw(key_list[4], (KW, HK * DK), KW ** -0.5, 3.0, ((1, 8),)),
        "key_conv": bell_draw(key_list[5], (KW, HK * DK), KW ** -0.5, 3.0, ((1, 8),)),
        "value_conv": bell_draw(key_list[6], (KW, HV * DV), KW ** -0.5, 3.0, ((1, 8),)),
        "beta_rate": draw_beta_rate(jax.random.fold_in(key_list[11], 71), 0),
        "log_decay": draw_log_decay(jax.random.fold_in(key_list[11], 71), 0),
        "norm_gain": jnp.clip(1.0 + 0.18 * jax.random.normal(key_list[9], (DV,), jnp.float32), 0.1, 1.9),
        "out_weight": bell_draw(key_list[10], (HV * DV, D), (HV * DV) ** -0.5, 0.09375, ((0, 8),)),
    }


precise = lax.Precision.HIGHEST

def pairwise_dot_entries(form, left, right):
    return jnp.einsum(form, left, right, precision=precise)

def causal_conv(rim_rows, raw_rows, tap_weights):
    joined = jnp.concatenate([rim_rows, raw_rows], axis=0).astype(jnp.float32)
    taps = tap_weights.astype(jnp.float32)
    row_count = raw_rows.shape[0]
    running = taps[0] * joined[0:row_count]
    for offset in range(1, tap_weights.shape[0]):
        running = running + taps[offset] * joined[offset:offset + row_count]
    return jax.nn.silu(running)

def unit_rows(key_rows):
    return key_rows * lax.rsqrt(lax.optimization_barrier(jnp.sum(key_rows * key_rows, axis=-1, keepdims=True)) + 1e-06)

def block_prep(probe_vectors, key_rows, values, strength, decay):
    block_size = decay.shape[-1]
    cumulative = jnp.cumsum(decay, axis=-1)
    row_index = lax.broadcasted_iota(jnp.int32, (block_size, block_size), 0)
    col_index = lax.broadcasted_iota(jnp.int32, (block_size, block_size), 1)
    spread = cumulative[..., :, None] - cumulative[..., None, :]
    fading = jnp.where(row_index >= col_index, jnp.exp(jnp.minimum(spread, 0.0)), 0.0)
    inner_dots = pairwise_dot_entries('...ik,...jk->...ij', key_rows, key_rows)
    lower_part = jnp.where(row_index > col_index, strength[..., :, None] * fading * inner_dots, 0.0)
    unit_lower = jnp.eye(block_size, dtype=jnp.float32) + lower_part
    cumulative_forget_ratio = jnp.exp(cumulative)
    stacked = jnp.concatenate([strength[..., None] * values, (strength * cumulative_forget_ratio)[..., None] * key_rows], axis=-1)
    solved = jax.scipy.linalg.solve_triangular(unit_lower, stacked, lower=True, unit_diagonal=True)
    value_width = values.shape[-1]
    state_updates = solved[..., :value_width]
    weight_params = solved[..., value_width:]
    causal_similarity_matrix = jnp.where(row_index >= col_index, fading * pairwise_dot_entries('...ik,...jk->...ij', probe_vectors, key_rows), 0.0)
    block_decay_factor = cumulative_forget_ratio[..., -1]
    decayed_tail_keys = jnp.exp(cumulative[..., -1:] - cumulative)[..., None] * key_rows
    return (probe_vectors, state_updates, weight_params, causal_similarity_matrix, cumulative_forget_ratio, decayed_tail_keys, block_decay_factor)

def block_step(running_recurrent_summary, block_data):
    probe_vectors, state_updates, weight_params, causal_similarity_matrix, cumulative_forget_ratio, decayed_tail_keys, block_decay_factor = block_data
    residual_target_vectors = state_updates - pairwise_dot_entries('ret,rtw->rew', weight_params, running_recurrent_summary)
    emitted_vectors = cumulative_forget_ratio[..., None] * pairwise_dot_entries('ret,rtw->rew', probe_vectors, running_recurrent_summary) + pairwise_dot_entries('keo,kov->kev', causal_similarity_matrix, residual_target_vectors)
    running_recurrent_summary = block_decay_factor[:, None, None] * running_recurrent_summary + pairwise_dot_entries('dwn,dwm->dnm', decayed_tail_keys, residual_target_vectors)
    return (running_recurrent_summary, emitted_vectors)

def gate_norm(core_out, gate_values, norm_gain):
    gate_part = gate_values.astype(jnp.float32).reshape(core_out.shape)
    scaling = lax.rsqrt(lax.optimization_barrier(jnp.mean(core_out * core_out, axis=-1, keepdims=True)) + 1e-06)
    gated = (core_out * scaling * norm_gain * jax.nn.silu(gate_part)).astype(jnp.bfloat16)
    return gated.reshape(core_out.shape[0], core_out.shape[1] * core_out.shape[2])

def reference(query_in, key_in, value_in, gate_values, query_conv, key_conv, value_conv, beta_rate, log_decay, norm_gain, out_weight):
    head_ratio = HV // HK
    block_count = TOKENS // BLOCK

    def convolve(raw_rows, tap_weights):
        rim_rows = jnp.zeros((tap_weights.shape[0] - 1, raw_rows.shape[1]), raw_rows.dtype)
        return causal_conv(rim_rows, raw_rows, tap_weights)
    probe_vectors = convolve(query_in, query_conv).reshape(block_count, BLOCK, HK, DK).transpose(0, 2, 1, 3)
    key_rows = unit_rows(convolve(key_in, key_conv).reshape(block_count, BLOCK, HK, DK)).transpose(0, 2, 1, 3)
    values = convolve(value_in, value_conv).reshape(block_count, BLOCK, HV, DV).transpose(0, 2, 1, 3)
    strength = beta_rate.reshape(HV, block_count, BLOCK).transpose(1, 0, 2)
    decay = log_decay.reshape(HV, block_count, BLOCK).transpose(1, 0, 2)

    def advance(running_recurrent_summary, block_data):
        query_block, key_block, value_block, strength_block, decay_block = block_data
        prepared = block_prep(jnp.repeat(query_block, head_ratio, axis=0), jnp.repeat(key_block, head_ratio, axis=0), value_block, strength_block, decay_block)
        return block_step(running_recurrent_summary, prepared)
    zero_state = jnp.zeros((HV, DK, DV), jnp.float32)
    final_state, emitted_vectors = lax.scan(advance, zero_state, (probe_vectors, key_rows, values, strength, decay))
    core_out = emitted_vectors.transpose(0, 2, 1, 3).reshape(TOKENS, HV, DV)
    gated = gate_norm(core_out, gate_values, norm_gain)
    group_cols = HV * DV // N_TP
    running = jnp.zeros((TOKENS, D), jnp.float32)
    for member in range(N_TP):
        partial_sum = jnp.dot(gated[:, member * group_cols:(member + 1) * group_cols].astype(jnp.float32), out_weight[member * group_cols:(member + 1) * group_cols].astype(jnp.float32), preferred_element_type=jnp.float32)
        rounded = lax.optimization_barrier(partial_sum.astype(jnp.bfloat16))
        running = running + rounded.astype(jnp.float32)
    return running.astype(jnp.bfloat16)
```

```python
import functools

import jax
import jax.numpy as jnp
from jax import lax
from jax.experimental import pallas as pl
from jax.experimental.pallas import tpu as pltpu
from jax.sharding import Mesh
from jax.sharding import PartitionSpec as P

DK = 128
DV = 128
F32 = jnp.float32
BF16 = jnp.bfloat16
INTERPRET = False

NN = (((1,), (0,)), ((), ()))
NT = (((1,), (1,)), ((), ()))
TN = (((0,), (0,)), ((), ()))


def dot(a, b, dims=NN):
    return lax.dot_general(a, b, dims, preferred_element_type=F32)


def split(x):
    high = x.astype(BF16)
    return high, (x - high.astype(F32)).astype(BF16)


def dot3(a, b, dims=NN):
    return dot(a[0], b[0], dims) + (dot(a[0], b[1], dims) + dot(a[1], b[0], dims))


def dot2(a, b, dims=NN):
    return dot(a[0], b, dims) + dot(a[1], b, dims)


def silu(x):
    return x / (1.0 + jnp.exp(-x))


def conv(rim, raw, taps):
    joined = jnp.concatenate([rim, raw], axis=0).astype(F32)
    taps = taps.astype(F32)
    rows = raw.shape[0]
    count = taps.shape[0]
    base = rim.shape[0] - (count - 1)
    running = taps[0:1] * joined[base : base + rows]
    for offset in range(1, count):
        running = running + taps[offset : offset + 1] * joined[base + offset : base + offset + rows]
    return silu(running)


def prepare_kernel(
    rim_ref, q_ref, k_ref, v_ref, qt_ref, kt_ref, vt_ref, beta_ref, decay_ref, maps_ref, base_ref, reach_ref
):
    rows = q_ref.shape[0]
    heads = beta_ref.shape[0]
    key_heads = q_ref.shape[1] // DK
    ratio = heads // key_heads
    q_cols = q_ref.shape[1]

    row = lax.broadcasted_iota(jnp.int32, (rows, rows), 0)
    col = lax.broadcasted_iota(jnp.int32, (rows, rows), 1)
    lower = row >= col
    strict = row > col
    ones = jnp.where(lower, 1.0, 0.0).astype(BF16)
    eye = jnp.where(row == col, 1.0, 0.0)
    eye_b = eye.astype(BF16)

    both = jnp.concatenate([decay_ref[...], beta_ref[...]], axis=0)
    high = both.astype(BF16)
    rest = both - high.astype(F32)
    mid = rest.astype(BF16)
    low = (rest - mid.astype(F32)).astype(BF16)
    upto_col = dot(ones, high, NT) + (dot(ones, mid, NT) + dot(ones, low, NT))
    upto_row = dot(high, ones, NT) + (dot(mid, ones, NT) + dot(low, ones, NT))
    plain_col = dot(eye_b, high, NT) + (dot(eye_b, mid, NT) + dot(eye_b, low, NT))

    keys = []
    inner = []
    cross = []
    queries = []
    for g in range(key_heads):
        cols = slice(g * DK, (g + 1) * DK)
        q = conv(rim_ref[:, cols], q_ref[:, cols], qt_ref[:, cols])
        k = conv(rim_ref[:, q_cols + g * DK : q_cols + (g + 1) * DK], k_ref[:, cols], kt_ref[:, cols])
        k = k * lax.rsqrt(jnp.sum(k * k, axis=-1, keepdims=True) + 1e-06)
        k_parts = split(k)
        queries.append(q)
        keys.append(k)
        inner.append(dot3(k_parts, k_parts, NT))
        cross.append(dot3(split(q), k_parts, NT))

    lowers = []
    solved = []
    sims = []
    for h in range(heads):
        g = h // ratio
        fading = jnp.where(lower, jnp.exp(jnp.minimum(upto_col[:, h : h + 1] - upto_row[h : h + 1, :], 0.0)), 0.0)
        beta = plain_col[:, heads + h : heads + h + 1]
        lower_part = jnp.where(strict, beta * fading * inner[g], 0.0)
        sims.append(split(fading * cross[g]))
        lowers.append(split(lower_part))
        solved.append(eye - jnp.where((row // 2 == col // 2), lower_part, 0.0))

    size = 2
    while size < rows:
        pick = (row // (2 * size) == col // (2 * size)) & (row // size > col // size)
        for h in range(heads):
            off = tuple(jnp.where(pick, part, jnp.zeros_like(part)) for part in lowers[h])
            x = split(solved[h])
            solved[h] = solved[h] - dot3(x, split(dot3(off, x)))
        size *= 2

    for h in range(heads):
        g = h // ratio
        vcols = slice(h * DV, (h + 1) * DV)
        start = q_cols * 2 + h * DV
        v = conv(rim_ref[:, start : start + DV], v_ref[:, vcols], vt_ref[:, vcols])
        beta = plain_col[:, heads + h : heads + h + 1]
        reach = jnp.exp(upto_col[:, h : h + 1])
        last = upto_col[rows - 1 : rows, h : h + 1]
        right = jnp.concatenate([(beta * reach) * keys[g], beta * v], axis=1)
        answer = split(dot3(split(solved[h]), split(right)))
        tail = jnp.exp(last - upto_col[:, h : h + 1]) * keys[g]
        folded = dot3(answer, split(tail), TN)
        emitted = dot3(sims[h], answer)
        base_ref[:, vcols] = emitted[:, DK:]
        reach_ref[:, vcols] = (reach * queries[g] - emitted[:, :DK]).astype(BF16)
        square = jnp.where(row[:DK, :DK] == col[:DK, :DK], jnp.exp(last), 0.0)
        step_map = (square - folded[:DK]).astype(BF16)
        added = folded[DK:].astype(BF16)
        half = DV // 2
        maps_ref[2 * h, :DK] = step_map
        maps_ref[2 * h + 1, :DK] = step_map
        maps_ref[2 * h, DK:] = added[:half]
        maps_ref[2 * h + 1, DK:] = added[half:]


def line_kernel(maps_ref, prefix_ref, total_ref):
    count = maps_ref.shape[0]
    rows = maps_ref.shape[1]
    row = lax.broadcasted_iota(jnp.int32, (rows, DK), 0)
    col = lax.broadcasted_iota(jnp.int32, (rows, DK), 1)
    prefix_ref[0] = jnp.where(row == col, 1.0, 0.0)
    running = maps_ref[0].astype(F32)
    for place in range(1, count):
        prefix_ref[place] = running
        added = jnp.where(row >= DK, maps_ref[place].astype(F32), 0.0)
        running = dot2(split(running), maps_ref[place, :DK]) + added
    total = running.astype(BF16)
    for place in range(total_ref.shape[0]):
        total_ref[place] = total


def start_kernel(place_ref, totals_ref, prefix_ref, state_ref):
    count = totals_ref.shape[0]
    place = place_ref[0]
    half = totals_ref.shape[1] - DK
    state = jnp.zeros((half, DK), F32)
    for earlier in range(count - 1):
        later = totals_ref[earlier, DK:].astype(F32)
        if earlier > 0:
            later = later + dot2(split(state), totals_ref[earlier, :DK])
        state = jnp.where(earlier < place, later, state)
    parts = split(state)
    for step in range(prefix_ref.shape[0]):
        moved = prefix_ref[step, DK:] + dot3(parts, split(prefix_ref[step, :DK]))
        state_ref[step] = moved.astype(BF16)


def finish_kernel(base_ref, reach_ref, state_ref, gate_ref, gain_ref, weight_ref, out_ref):
    heads = base_ref.shape[1] // DV
    gain = gain_ref[...]
    pieces = []
    for h in range(heads):
        cols = slice(h * DV, (h + 1) * DV)
        core = base_ref[:, cols] + dot(reach_ref[:, cols], state_ref[h], NT)
        scale = lax.rsqrt(jnp.mean(core * core, axis=-1, keepdims=True) + 1e-06)
        gate = silu(gate_ref[:, cols].astype(F32))
        pieces.append((core * scale * gain * gate).astype(BF16))
    gated = jnp.concatenate(pieces, axis=1)
    width = 512
    for start in range(0, out_ref.shape[1], width):
        cols = slice(start, start + width)
        out_ref[:, cols] = dot(gated, weight_ref[:, cols]).astype(BF16)


def call(kernel, outs, *args, scalars=0):
    vmem = pl.BlockSpec(memory_space=pltpu.VMEM)
    smem = pl.BlockSpec(memory_space=pltpu.SMEM)
    return pl.pallas_call(
        kernel,
        out_shape=outs,
        in_specs=[smem] * scalars + [vmem] * (len(args) - scalars),
        out_specs=jax.tree.map(lambda _: vmem, outs),
        compiler_params=pltpu.CompilerParams(vmem_limit_bytes=48 << 20),
        interpret=INTERPRET,
    )(*args)


def local(
    nz,
    ny,
    ntp,
    query_in,
    key_in,
    value_in,
    gate_values,
    query_conv,
    key_conv,
    value_conv,
    beta_rate,
    log_decay,
    norm_gain,
    out_weight,
):
    shape = jax.ShapeDtypeStruct
    rows = query_in.shape[0]
    heads = beta_rate.shape[0]
    rim = 16
    tail_rows = jnp.concatenate([a[rows - rim :] for a in (query_in, key_in, value_in)], axis=1)
    count = nz * ny
    rim_rows = lax.ppermute(tail_rows, ("z", "y"), [(i, i + 1) for i in range(count - 1)])

    half = DV // 2
    maps, base, reach = call(
        prepare_kernel,
        (
            shape((2 * heads, DK + half, DK), BF16),
            shape((rows, heads * DV), F32),
            shape((rows, heads * DK), BF16),
        ),
        rim_rows, query_in, key_in, value_in, query_conv, key_conv, value_conv, beta_rate, log_decay,
    )
    maps = lax.all_to_all(maps, "y", 0, 0, tiled=True)
    prefix, totals = call(
        line_kernel, (shape((ny, DK + half, DK), F32), shape((nz, DK + half, DK), BF16)), maps
    )
    totals = lax.all_to_all(totals, "z", 0, 0, tiled=True)
    place = lax.axis_index("z").reshape(1).astype(jnp.int32)
    states = call(start_kernel, shape((ny, half, DK), BF16), place, totals, prefix, scalars=1)
    states = lax.all_to_all(states, "y", 0, 0, tiled=True)
    partial = call(
        finish_kernel,
        shape((rows, out_weight.shape[1]), BF16),
        base, reach, states.reshape(heads, DV, DK), gate_values, norm_gain.reshape(1, DV), out_weight,
    )
    parts = lax.all_to_all(partial.reshape(ntp, rows // ntp, -1), "tp", 0, 0, tiled=True)
    return jnp.sum(parts.astype(F32), axis=0).astype(BF16)


def build(mesh):
    nz, ny, ntp = mesh.devices.shape
    ctx = ("z", "y")
    return jax.shard_map(
        functools.partial(local, nz, ny, ntp),
        mesh=mesh,
        in_specs=(
            P(ctx, "tp"),
            P(ctx, "tp"),
            P(ctx, "tp"),
            P(ctx, "tp"),
            P(None, "tp"),
            P(None, "tp"),
            P(None, "tp"),
            P("tp", ctx),
            P("tp", ctx),
            P(),
            P("tp", None),
        ),
        out_specs=P((*ctx, "tp"), None),
        check_vma=False,
    )


def solution(mesh):
    return build(Mesh(mesh.devices.reshape(8, 8, 8), ("z", "y", "tp")))
```

```python
import functools

import jax
import jax.numpy as jnp
from jax import lax
from jax.experimental import pallas as pl
from jax.experimental.pallas import tpu as pltpu
from jax.sharding import Mesh
from jax.sharding import PartitionSpec as P

DK = 128
DV = 128
F32 = jnp.float32
BF16 = jnp.bfloat16
INTERPRET = False
REACH_LIMIT = 60

NN = (((1,), (0,)), ((), ()))
NT = (((1,), (1,)), ((), ()))
TN = (((0,), (0,)), ((), ()))


def dot(a, b, dims=NN):
    return lax.dot_general(a, b, dims, preferred_element_type=F32)


def split(x):
    high = x.astype(BF16)
    return high, (x - high.astype(F32)).astype(BF16)


def dot3(a, b, dims=NN):
    return dot(a[0], b[0], dims) + (dot(a[0], b[1], dims) + dot(a[1], b[0], dims))


def dot2(a, b, dims=NN):
    return dot(a[0], b, dims) + dot(a[1], b, dims)


def silu(x):
    return x / (1.0 + jnp.exp(-x))


def conv(rim, raw, taps):
    joined = jnp.concatenate([rim, raw], axis=0).astype(F32)
    taps = taps.astype(F32)
    rows = raw.shape[0]
    count = taps.shape[0]
    base = rim.shape[0] - (count - 1)
    running = taps[0:1] * joined[base : base + rows]
    for offset in range(1, count):
        running = running + taps[offset : offset + 1] * joined[base + offset : base + offset + rows]
    return silu(running)


def fetch(pairs, sems):
    copies = [pltpu.make_async_copy(src, dst, sems.at[i]) for i, (src, dst) in enumerate(pairs)]
    for copy in copies:
        copy.start()
    return copies


def tail_kernel(q_hbm, k_hbm, v_hbm, out_ref, sems):
    rows = q_hbm.shape[0]
    count = out_ref.shape[0]
    start = 0
    pairs = []
    for source in (q_hbm, k_hbm, v_hbm):
        width = source.shape[1]
        pairs.append((source.at[pl.ds(rows - count, count)], out_ref.at[:, pl.ds(start, width)]))
        start += width
    for copy in fetch(pairs, sems):
        copy.wait()


def wide_left(parts):
    return jnp.concatenate(parts, axis=1)


def wide_right(parts):
    high, low = parts
    top = jnp.concatenate([high, low], axis=1)
    return jnp.concatenate([top, jnp.concatenate([high, jnp.zeros_like(low)], axis=1)], axis=0)


def packed(left, right):
    both = dot(left, right)
    width = both.shape[1] // 2
    return both[:, :width] + both[:, width:]


def triangle(shape):
    row = lax.broadcasted_iota(jnp.int32, shape, 0)
    col = lax.broadcasted_iota(jnp.int32, shape, 1)
    return row, col


def exact_sums(left, value, dims, swap):
    high = value.astype(BF16)
    rest = value - high.astype(F32)
    mid = rest.astype(BF16)
    low = (rest - mid.astype(F32)).astype(BF16)
    parts = [dot(p, left, dims) if swap else dot(left, p, dims) for p in (high, mid, low)]
    return parts[0] + (parts[1] + parts[2])


def prepare_kernel(
    rim_hbm,
    k_hbm,
    v_hbm,
    kt_hbm,
    vt_hbm,
    beta_hbm,
    decay_hbm,
    maps_hbm,
    answer_hbm,
    keys_hbm,
    rim_ref,
    k_ref,
    v_ref,
    kt_ref,
    vt_ref,
    beta_ref,
    decay_ref,
    maps_ref,
    answer_ref,
    keys_ref,
    sems,
    out_sems,
):
    copies = fetch(
        (
            (decay_hbm, decay_ref),
            (beta_hbm, beta_ref),
            (rim_hbm, rim_ref),
            (kt_hbm, kt_ref),
            (k_hbm, k_ref),
            (vt_hbm, vt_ref),
            (v_hbm, v_ref),
        ),
        sems,
    )
    sends = []

    def send(src, dst):
        copy = pltpu.make_async_copy(src, dst, out_sems.at[len(sends)])
        copy.start()
        sends.append(copy)

    rows = k_ref.shape[0]
    heads = beta_ref.shape[0]
    k_cols = k_ref.shape[1]
    key_heads = k_cols // DK
    ratio = heads // key_heads
    side = rows // 2

    row, col = triangle((side, side))
    strict = row > col
    eye = jnp.where(row == col, 1.0, 0.0)
    wide_row, wide_col = triangle((rows, rows))
    ones = jnp.where(wide_row >= wide_col, 1.0, 0.0).astype(BF16)
    eye_b = jnp.where(wide_row == wide_col, 1.0, 0.0).astype(BF16)

    copies[0].wait()
    copies[1].wait()
    both = jnp.concatenate([decay_ref[...], beta_ref[...]], axis=0)
    upto_col = exact_sums(ones, both, NT, False)
    upto_row = exact_sums(ones, both, NT, True)
    plain_col = exact_sums(eye_b, both, NT, False)

    keys = []
    inner = []
    for copy in copies[2:5]:
        copy.wait()
    for g in range(key_heads):
        cols = slice(g * DK, (g + 1) * DK)
        k = conv(rim_ref[:, k_cols + g * DK : k_cols + (g + 1) * DK], k_ref[:, cols], kt_ref[:, cols])
        k = k * lax.rsqrt(jnp.sum(k * k, axis=-1, keepdims=True) + 1e-06)
        keys.append(k)
        parts = split(k)
        keys_ref[:, cols] = parts[0]
        inner.append(dot3(parts, parts, NT))
    send(keys_ref, keys_hbm)

    spans = (slice(0, side), slice(side, rows))
    lowers = []
    solved = []
    for h in range(heads):
        g = h // ratio
        part = {}
        for i, j in ((0, 0), (1, 0), (1, 1)):
            spread = upto_col[spans[i], h : h + 1] - upto_row[h : h + 1, spans[j]]
            scaled = plain_col[spans[i], heads + h : heads + h + 1] * jnp.exp(jnp.minimum(spread, 0.0))
            value = scaled * inner[g][spans[i], spans[j]]
            part[i, j] = jnp.where(strict, value, 0.0) if i == j else value
        lowers.append({key: split(value) for key, value in part.items()})
        solved.append([eye - jnp.where(row // 2 == col // 2, part[d, d], 0.0) for d in range(2)])

    copies[5].wait()
    copies[6].wait()
    half = DV // 2
    lasts = [upto_col[rows - 1 : rows, h : h + 1] for h in range(heads)]
    rights = []
    tails = []

    def ready(h):
        g = h // ratio
        vcols = slice(h * DV, (h + 1) * DV)
        start = k_cols * 2 + h * DV
        v = conv(rim_ref[:, start : start + DV], v_ref[:, vcols], vt_ref[:, vcols])
        beta = plain_col[:, heads + h : heads + h + 1]
        reach = jnp.exp(upto_col[:, h : h + 1])
        rights.append(split(jnp.concatenate([(beta * reach) * keys[g], beta * v], axis=1)))
        tails.append(split(jnp.exp(lasts[h] - upto_col[:, h : h + 1]) * keys[g]))

    size = 2
    while size < side:
        pick = (row // (2 * size) == col // (2 * size)) & (row // size > col // size)
        middle = []
        for h in range(heads):
            for d in range(2):
                off = [jnp.where(pick, part, jnp.zeros_like(part)) for part in lowers[h][d, d]]
                x = split(solved[h][d])
                middle.append((x, packed(wide_left(off), wide_right(x))))
        if len(rights) < heads:
            ready(len(rights))
        for h in range(heads):
            for d in range(2):
                x, y = middle[2 * h + d]
                solved[h][d] = solved[h][d] - packed(wide_left(x), wide_right(split(y)))
        size *= 2
    while len(rights) < heads:
        ready(len(rights))

    done = [[split(x) for x in pair] for pair in solved]
    middle = [packed(wide_left(lowers[h][1, 0]), wide_right(done[h][0])) for h in range(heads)]
    firsts = []
    for h in range(heads):
        x0, right = done[h][0], rights[h]
        doubled = jnp.concatenate([right[0][:side]] * 2, axis=0)
        firsts.append(dot(wide_left(x0), doubled) + dot(x0[0], right[1][:side]))
    corners = [split(-packed(wide_left(done[h][1]), wide_right(split(middle[h])))) for h in range(heads)]
    answers = []
    for h in range(heads):
        bottom = [jnp.concatenate([corners[h][i], done[h][1][i]], axis=1) for i in range(2)]
        answers.append(split(jnp.concatenate([firsts[h], dot3(bottom, rights[h])], axis=0)))
        answer_ref[h] = answers[h][0]
        send(answer_ref.at[h], answer_hbm.at[h])
    folds = []
    for h in range(heads):
        folded = dot(answers[h][0], jnp.concatenate(tails[h], axis=1), TN)
        folds.append(folded[:, :DK] + (folded[:, DK:] + dot(answers[h][1], tails[h][0], TN)))
    for h in range(heads):
        square = jnp.where(row[:DK, :DK] == col[:DK, :DK], jnp.exp(lasts[h]), 0.0)
        step_map = (square - folds[h][:DK]).astype(BF16)
        added = folds[h][DK:].astype(BF16)
        maps_ref[2 * h, :DK] = step_map
        maps_ref[2 * h + 1, :DK] = step_map
        maps_ref[2 * h, DK:] = added[:half]
        maps_ref[2 * h + 1, DK:] = added[half:]
        send(maps_ref.at[pl.ds(2 * h, 2)], maps_hbm.at[pl.ds(2 * h, 2)])
    for copy in sends:
        copy.wait()


def reach_kernel(rim_ref, q_ref, qt_ref, decay_ref, answer_ref, keys_ref, base_ref, reach_ref):
    rows = q_ref.shape[0]
    heads = decay_ref.shape[0]
    key_heads = q_ref.shape[1] // DK
    ratio = heads // key_heads
    side = rows // 2
    row, col = triangle((side, side))
    lower = row >= col
    wide_row, wide_col = triangle((rows, rows))
    ones = jnp.where(wide_row >= wide_col, 1.0, 0.0).astype(BF16)
    both = jnp.concatenate([decay_ref[...], decay_ref[...]], axis=0)
    upto_col = exact_sums(ones, both, NT, False)
    upto_row = exact_sums(ones, both, NT, True)
    queries = []
    cross = []
    for g in range(key_heads):
        cols = slice(g * DK, (g + 1) * DK)
        q = conv(rim_ref[:, cols], q_ref[:, cols], qt_ref[:, cols])
        queries.append(q)
        cross.append(dot(q.astype(BF16), keys_ref[:, cols], NT))
    spans = (slice(0, side), slice(side, rows))
    for h in range(heads):
        g = h // ratio
        vcols = slice(h * DV, (h + 1) * DV)
        sims = {}
        for i, j in ((0, 0), (1, 0), (1, 1)):
            spread = upto_col[spans[i], h : h + 1] - upto_row[h : h + 1, spans[j]]
            value = jnp.exp(jnp.minimum(spread, 0.0)) * cross[g][spans[i], spans[j]]
            sims[i, j] = (jnp.where(lower, value, 0.0) if i == j else value).astype(BF16)
        for i in range(2):
            left = sims[0, 0] if i == 0 else jnp.concatenate([sims[1, 0], sims[1, 1]], axis=1)
            emitted = dot(left, answer_ref[h, : left.shape[1]])
            base_ref[spans[i], vcols] = emitted[:, DK:]
            gone = jnp.exp(upto_col[spans[i], h : h + 1])
            reach_ref[spans[i], vcols] = (gone * queries[g][spans[i]] - emitted[:, :DK]).astype(BF16)


def line_kernel(maps_ref, prefix_ref, total_ref):
    count = maps_ref.shape[0]
    rows = maps_ref.shape[1]
    row = lax.broadcasted_iota(jnp.int32, (rows, DK), 0)
    col = lax.broadcasted_iota(jnp.int32, (rows, DK), 1)
    prefix_ref[0] = jnp.where(row == col, 1.0, 0.0)
    running = maps_ref[0].astype(F32)
    for place in range(1, count):
        prefix_ref[place] = running
        added = jnp.where(row >= DK, maps_ref[place].astype(F32), 0.0)
        running = dot2(split(running), maps_ref[place, :DK]) + added
    total = running.astype(BF16)
    for place in range(total_ref.shape[0]):
        total_ref[place] = total


def start_kernel(totals_ref, prefix_ref, state_ref):
    count = totals_ref.shape[0]
    place = lax.axis_index("z")
    half = totals_ref.shape[1] - DK
    state = jnp.zeros((half, DK), F32)
    for earlier in range(count - 1):
        later = totals_ref[earlier, DK:].astype(F32)
        if earlier > 0:
            later = later + dot2(split(state), totals_ref[earlier, :DK])
        state = jnp.where(earlier < place, later, state)
    parts = split(state)
    for step in range(prefix_ref.shape[0]):
        moved = prefix_ref[step, DK:] + dot3(parts, split(prefix_ref[step, :DK]))
        state_ref[step] = moved.astype(BF16)


def finish_kernel(base_ref, reach_ref, state_ref, gate_ref, gain_ref, weight_ref, out_ref):
    heads = base_ref.shape[1] // DV
    gain = gain_ref[...]
    pieces = []
    for h in range(heads):
        cols = slice(h * DV, (h + 1) * DV)
        core = base_ref[:, cols] + dot(reach_ref[:, cols], state_ref[h], NT)
        scale = lax.rsqrt(jnp.mean(core * core, axis=-1, keepdims=True) + 1e-06)
        gate = silu(gate_ref[:, cols].astype(F32))
        pieces.append((core * scale * gain * gate).astype(BF16))
    gated = jnp.concatenate(pieces, axis=1)
    width = 512
    for start in range(0, out_ref.shape[1], width):
        cols = slice(start, start + width)
        out_ref[:, cols] = dot(gated, weight_ref[:, cols]).astype(BF16)


def call(kernel, outs, *args, hbm=(), hbm_outs=False, scratch=(), limit=24):
    vmem = pl.BlockSpec(memory_space=pltpu.VMEM)
    far = pl.BlockSpec(memory_space=pltpu.HBM)
    return pl.pallas_call(
        kernel,
        out_shape=outs,
        in_specs=[far if i in hbm else vmem for i in range(len(args))],
        out_specs=jax.tree.map(lambda _: far if hbm_outs else vmem, outs),
        scratch_shapes=list(scratch),
        compiler_params=pltpu.CompilerParams(vmem_limit_bytes=limit << 20),
        interpret=pltpu.InterpretParams() if INTERPRET else False,
    )(*args)


def local(
    nz,
    ny,
    ntp,
    query_in,
    key_in,
    value_in,
    gate_values,
    query_conv,
    key_conv,
    value_conv,
    beta_rate,
    log_decay,
    norm_gain,
    out_weight,
):
    shape = jax.ShapeDtypeStruct
    rows = query_in.shape[0]
    heads = beta_rate.shape[0]
    rim = 16
    raw = (query_in, key_in, value_in)
    tail_rows = call(
        tail_kernel,
        shape((rim, sum(a.shape[1] for a in raw)), BF16),
        *raw,
        hbm=range(3),
        scratch=(pltpu.SemaphoreType.DMA((3,)),),
        limit=60,
    )
    count = nz * ny
    rim_rows = lax.ppermute(tail_rows, ("z", "y"), [(i, i + 1) for i in range(count - 1)])

    half = DV // 2
    inputs = (rim_rows, key_in, value_in, key_conv, value_conv, beta_rate, log_decay)
    made = (
        shape((2 * heads, DK + half, DK), BF16),
        shape((heads, rows, DK + DV), BF16),
        shape(key_in.shape, BF16),
    )
    maps, answer, keys = call(
        prepare_kernel,
        made,
        *inputs,
        hbm=range(len(inputs)),
        hbm_outs=True,
        scratch=(
            *(pltpu.VMEM(a.shape, a.dtype) for a in (*inputs, *made)),
            pltpu.SemaphoreType.DMA((len(inputs),)),
            pltpu.SemaphoreType.DMA((2 * heads + 1,)),
        ),
        limit=60,
    )
    base, reach = call(
        reach_kernel,
        (shape((rows, heads * DV), F32), shape((rows, heads * DK), BF16)),
        rim_rows,
        query_in,
        query_conv,
        log_decay,
        answer,
        keys,
        limit=REACH_LIMIT,
    )
    maps = lax.all_to_all(maps, "y", 0, 0, tiled=True)
    maps, base, reach = lax.optimization_barrier((maps, base, reach))
    prefix, totals = call(
        line_kernel, (shape((ny, DK + half, DK), F32), shape((nz, DK + half, DK), BF16)), maps
    )
    totals = lax.all_to_all(totals, "z", 0, 0, tiled=True)
    states = call(start_kernel, shape((ny, half, DK), BF16), totals, prefix)
    states = lax.all_to_all(states, "y", 0, 0, tiled=True)
    partial = call(
        finish_kernel,
        shape((rows, out_weight.shape[1]), BF16),
        base,
        reach,
        states.reshape(heads, DV, DK),
        gate_values,
        norm_gain.reshape(1, DV),
        out_weight,
    )
    parts = lax.all_to_all(partial.reshape(ntp, rows // ntp, -1), "tp", 0, 0, tiled=True)
    return jnp.sum(parts.astype(F32), axis=0).astype(BF16)


def build(mesh):
    nz, ny, ntp = mesh.devices.shape
    ctx = ("z", "y")
    return jax.shard_map(
        functools.partial(local, nz, ny, ntp),
        mesh=mesh,
        in_specs=(
            P(ctx, "tp"),
            P(ctx, "tp"),
            P(ctx, "tp"),
            P(ctx, "tp"),
            P(None, "tp"),
            P(None, "tp"),
            P(None, "tp"),
            P("tp", ctx),
            P("tp", ctx),
            P(),
            P("tp", None),
        ),
        out_specs=P((*ctx, "tp"), None),
        check_vma=False,
    )


def solution(mesh):
    return build(Mesh(mesh.devices.reshape(8, 8, 8), ("z", "y", "tp")))
```

```python
import functools

import jax
import jax.numpy as jnp
from jax import lax
from jax.experimental import pallas as pl
from jax.experimental.pallas import tpu as pltpu
from jax.sharding import Mesh
from jax.sharding import PartitionSpec as P

DK = 128
DV = 128
F32 = jnp.float32
BF16 = jnp.bfloat16
INTERPRET = False
REACH_LIMIT = 60

NN = (((1,), (0,)), ((), ()))
NT = (((1,), (1,)), ((), ()))
TN = (((0,), (0,)), ((), ()))


def dot(a, b, dims=NN):
    return lax.dot_general(a, b, dims, preferred_element_type=F32)


def split(x):
    high = x.astype(BF16)
    return high, (x - high.astype(F32)).astype(BF16)


def dot3(a, b, dims=NN):
    return dot(a[0], b[0], dims) + (dot(a[0], b[1], dims) + dot(a[1], b[0], dims))


def dot2(a, b, dims=NN):
    return dot(a[0], b, dims) + dot(a[1], b, dims)


def silu(x):
    return x / (1.0 + jnp.exp(-x))


def conv(rim, raw, taps):
    joined = jnp.concatenate([rim, raw], axis=0).astype(F32)
    taps = taps.astype(F32)
    rows = raw.shape[0]
    count = taps.shape[0]
    base = rim.shape[0] - (count - 1)
    running = taps[0:1] * joined[base : base + rows]
    for offset in range(1, count):
        running = running + taps[offset : offset + 1] * joined[base + offset : base + offset + rows]
    return silu(running)


def fetch(pairs, sems):
    copies = [pltpu.make_async_copy(src, dst, sems.at[i]) for i, (src, dst) in enumerate(pairs)]
    for copy in copies:
        copy.start()
    return copies


def tail_kernel(q_hbm, k_hbm, v_hbm, out_ref, sems):
    rows = q_hbm.shape[0]
    count = out_ref.shape[0]
    start = 0
    pairs = []
    for source in (q_hbm, k_hbm, v_hbm):
        width = source.shape[1]
        pairs.append((source.at[pl.ds(rows - count, count)], out_ref.at[:, pl.ds(start, width)]))
        start += width
    for copy in fetch(pairs, sems):
        copy.wait()


def wide_left(parts):
    return jnp.concatenate(parts, axis=1)


def wide_right(parts):
    high, low = parts
    top = jnp.concatenate([high, low], axis=1)
    return jnp.concatenate([top, jnp.concatenate([high, jnp.zeros_like(low)], axis=1)], axis=0)


def packed(left, right):
    both = dot(left, right)
    width = both.shape[1] // 2
    return both[:, :width] + both[:, width:]


def triangle(shape):
    row = lax.broadcasted_iota(jnp.int32, shape, 0)
    col = lax.broadcasted_iota(jnp.int32, shape, 1)
    return row, col


def pieces(value):
    high = value.astype(BF16).astype(F32)
    rest = value - high
    mid = rest.astype(BF16).astype(F32)
    return jnp.concatenate([high, mid, rest - mid], axis=0).astype(BF16)


def column_sums(left, parts):
    wide = dot(left, parts, NT)
    count = wide.shape[1] // 3
    return wide[:, :count] + (wide[:, count : 2 * count] + wide[:, 2 * count :])


def row_sums(left, parts):
    tall = dot(parts, left, NT)
    count = tall.shape[0] // 3
    return tall[:count] + (tall[count : 2 * count] + tall[2 * count :])


def clock(decay_ref, beta_ref, rows):
    row, col = triangle((rows, rows))
    ones = jnp.where(row >= col, 1.0, 0.0).astype(BF16)
    eye = jnp.where(row == col, 1.0, 0.0).astype(BF16)
    parts = pieces(jnp.concatenate([decay_ref[...], beta_ref[...]], axis=0))
    return column_sums(ones, parts), row_sums(ones, parts), column_sums(eye, parts)


def lower_block(upto_col, upto_row, plain_col, inner, h, heads, rows, cols):
    spread = upto_col[rows, h : h + 1] - upto_row[h : h + 1, cols]
    scaled = plain_col[rows, heads + h : heads + h + 1] * jnp.exp(jnp.minimum(spread, 0.0))
    return scaled * inner


def unit(rows_of_keys):
    return rows_of_keys * lax.rsqrt(jnp.sum(rows_of_keys * rows_of_keys, axis=-1, keepdims=True) + 1e-06)


def level_masks(side):
    row, col = triangle((side, side))
    size = 2
    while size < side:
        yield (row // (2 * size) == col // (2 * size)) & (row // size > col // size)
        size *= 2


def start_inverse(lower):
    row, col = triangle(lower.shape)
    return jnp.where(row == col, 1.0, 0.0) - jnp.where(row // 2 == col // 2, lower, 0.0)


def half_level(pick, lower, solved):
    off = [jnp.where(pick, part, jnp.zeros_like(part)) for part in lower]
    x = split(solved)
    return x, packed(wide_left(off), wide_right(x))


def first_kernel(
    k_hbm,
    v_hbm,
    kt_hbm,
    vt_hbm,
    keys_hbm,
    values_hbm,
    k_ref,
    v_ref,
    kt_ref,
    vt_ref,
    keys_ref,
    values_ref,
    sems,
    out_sems,
):
    copies = fetch(((kt_hbm, kt_ref), (k_hbm, k_ref), (vt_hbm, vt_ref), (v_hbm, v_ref)), sems)
    empty = jnp.zeros((16, DK), BF16)
    copies[0].wait()
    copies[1].wait()
    for start in range(0, k_ref.shape[1], DK):
        cols = slice(start, start + DK)
        keys_ref[:, cols] = unit(conv(empty, k_ref[:, cols], kt_ref[:, cols]))
    sends = [pltpu.make_async_copy(keys_ref, keys_hbm, out_sems.at[0])]
    sends[0].start()
    copies[2].wait()
    copies[3].wait()
    for start in range(0, v_ref.shape[1], DV):
        cols = slice(start, start + DV)
        values_ref[:, cols] = conv(empty, v_ref[:, cols], vt_ref[:, cols])
    sends.append(pltpu.make_async_copy(values_ref, values_hbm, out_sems.at[1]))
    sends[1].start()
    for copy in sends:
        copy.wait()


def prepare_kernel(
    rim_hbm,
    kt_hbm,
    vt_hbm,
    beta_hbm,
    decay_hbm,
    keys_hbm,
    values_hbm,
    k_hbm,
    v_hbm,
    maps_hbm,
    answer_hbm,
    keys_out_hbm,
    rim_ref,
    kt_ref,
    vt_ref,
    beta_ref,
    decay_ref,
    made_keys_ref,
    made_values_ref,
    k_ref,
    v_ref,
    maps_ref,
    answer_ref,
    keys_ref,
    sems,
    out_sems,
):
    rim = rim_ref.shape[0]
    copies = fetch(
        (
            (decay_hbm, decay_ref),
            (beta_hbm, beta_ref),
            (rim_hbm, rim_ref),
            (kt_hbm, kt_ref),
            (k_hbm.at[pl.ds(0, rim)], k_ref),
            (keys_hbm, made_keys_ref),
            (vt_hbm, vt_ref),
            (v_hbm.at[pl.ds(0, rim)], v_ref),
            (values_hbm, made_values_ref),
        ),
        sems,
    )
    sends = []

    def send(src, dst):
        copy = pltpu.make_async_copy(src, dst, out_sems.at[len(sends)])
        copy.start()
        sends.append(copy)

    rows = made_keys_ref.shape[0]
    heads = beta_ref.shape[0]
    k_cols = made_keys_ref.shape[1]
    key_heads = k_cols // DK
    ratio = heads // key_heads
    side = rows // 2
    row, col = triangle((side, side))

    copies[0].wait()
    copies[1].wait()
    upto_col, upto_row, plain_col = clock(decay_ref, beta_ref, rows)

    keys = []
    inner = []
    for copy in copies[2:6]:
        copy.wait()
    for g in range(key_heads):
        cols = slice(g * DK, (g + 1) * DK)
        top = unit(conv(rim_ref[:, k_cols + g * DK : k_cols + (g + 1) * DK], k_ref[:, cols], kt_ref[:, cols]))
        k = jnp.concatenate([top, made_keys_ref[rim:, cols]], axis=0)
        keys.append(k)
        parts = split(k)
        keys_ref[:, cols] = parts[0]
        inner.append(dot3(parts, parts, NT))
    send(keys_ref, keys_out_hbm)

    spans = (slice(0, side), slice(side, rows))
    lowers = []
    solved = []
    for h in range(heads):
        part = {}
        for i, j in ((0, 0), (1, 0), (1, 1)):
            block = inner[h // ratio][spans[i], spans[j]]
            value = lower_block(upto_col, upto_row, plain_col, block, h, heads, spans[i], spans[j])
            part[i, j] = jnp.where(row > col, value, 0.0) if i == j else value
        lowers.append({key: split(value) for key, value in part.items()})
        solved.append([start_inverse(part[d, d]) for d in range(2)])

    for copy in copies[6:]:
        copy.wait()
    half = DV // 2
    lasts = [upto_col[rows - 1 : rows, h : h + 1] for h in range(heads)]
    rights = []
    tails = []

    def ready(h):
        g = h // ratio
        vcols = slice(h * DV, (h + 1) * DV)
        start = k_cols * 2 + h * DV
        top = conv(rim_ref[:, start : start + DV], v_ref[:, vcols], vt_ref[:, vcols])
        v = jnp.concatenate([top, made_values_ref[rim:, vcols]], axis=0)
        beta = plain_col[:, heads + h : heads + h + 1]
        reach = jnp.exp(upto_col[:, h : h + 1])
        rights.append(split(jnp.concatenate([(beta * reach) * keys[g], beta * v], axis=1)))
        tails.append(split(jnp.exp(lasts[h] - upto_col[:, h : h + 1]) * keys[g]))

    units = [(h, d) for h in range(heads) for d in range(2)]
    for pick in level_masks(side):
        middle = [half_level(pick, lowers[h][d, d], solved[h][d]) for h, d in units]
        if len(rights) < heads:
            ready(len(rights))
        for (h, d), (x, y) in zip(units, middle):
            solved[h][d] = solved[h][d] - packed(wide_left(x), wide_right(split(y)))
    while len(rights) < heads:
        ready(len(rights))

    done = [[split(x) for x in pair] for pair in solved]
    middle = [packed(wide_left(lowers[h][1, 0]), wide_right(done[h][0])) for h in range(heads)]
    firsts = []
    for h in range(heads):
        x0, right = done[h][0], rights[h]
        doubled = jnp.concatenate([right[0][:side]] * 2, axis=0)
        firsts.append(dot(wide_left(x0), doubled) + dot(x0[0], right[1][:side]))
    corners = [split(-packed(wide_left(done[h][1]), wide_right(split(middle[h])))) for h in range(heads)]
    answers = []
    for h in range(heads):
        bottom = [jnp.concatenate([corners[h][i], done[h][1][i]], axis=1) for i in range(2)]
        answers.append(split(jnp.concatenate([firsts[h], dot3(bottom, rights[h])], axis=0)))
        answer_ref[h] = answers[h][0]
        send(answer_ref.at[h], answer_hbm.at[h])
    folds = []
    for h in range(heads):
        folded = dot(answers[h][0], jnp.concatenate(tails[h], axis=1), TN)
        folds.append(folded[:, :DK] + (folded[:, DK:] + dot(answers[h][1], tails[h][0], TN)))
    for h in range(heads):
        square = jnp.where(row[:DK, :DK] == col[:DK, :DK], jnp.exp(lasts[h]), 0.0)
        step_map = (square - folds[h][:DK]).astype(BF16)
        added = folds[h][DK:].astype(BF16)
        maps_ref[2 * h, :DK] = step_map
        maps_ref[2 * h + 1, :DK] = step_map
        maps_ref[2 * h, DK:] = added[:half]
        maps_ref[2 * h + 1, DK:] = added[half:]
        send(maps_ref.at[pl.ds(2 * h, 2)], maps_hbm.at[pl.ds(2 * h, 2)])
    for copy in sends:
        copy.wait()


def reach_kernel(rim_ref, q_ref, qt_ref, decay_ref, answer_ref, keys_ref, base_ref, reach_ref):
    rows = q_ref.shape[0]
    heads = decay_ref.shape[0]
    key_heads = q_ref.shape[1] // DK
    ratio = heads // key_heads
    side = rows // 2
    row, col = triangle((side, side))
    lower = row >= col
    wide_row, wide_col = triangle((rows, rows))
    ones = jnp.where(wide_row >= wide_col, 1.0, 0.0).astype(BF16)
    parts = pieces(jnp.concatenate([decay_ref[...], decay_ref[...]], axis=0))
    upto_col = column_sums(ones, parts)
    upto_row = row_sums(ones, parts)
    queries = []
    cross = []
    for g in range(key_heads):
        cols = slice(g * DK, (g + 1) * DK)
        q = conv(rim_ref[:, cols], q_ref[:, cols], qt_ref[:, cols])
        queries.append(q)
        cross.append(dot(q.astype(BF16), keys_ref[:, cols], NT))
    spans = (slice(0, side), slice(side, rows))
    for h in range(heads):
        g = h // ratio
        vcols = slice(h * DV, (h + 1) * DV)
        sims = {}
        for i, j in ((0, 0), (1, 0), (1, 1)):
            spread = upto_col[spans[i], h : h + 1] - upto_row[h : h + 1, spans[j]]
            value = jnp.exp(jnp.minimum(spread, 0.0)) * cross[g][spans[i], spans[j]]
            sims[i, j] = (jnp.where(lower, value, 0.0) if i == j else value).astype(BF16)
        for i in range(2):
            left = sims[0, 0] if i == 0 else jnp.concatenate([sims[1, 0], sims[1, 1]], axis=1)
            emitted = dot(left, answer_ref[h, : left.shape[1]])
            base_ref[spans[i], vcols] = emitted[:, DK:]
            gone = jnp.exp(upto_col[spans[i], h : h + 1])
            reach_ref[spans[i], vcols] = (gone * queries[g][spans[i]] - emitted[:, :DK]).astype(BF16)


def line_kernel(maps_ref, prefix_ref, total_ref):
    count = maps_ref.shape[0]
    rows = maps_ref.shape[1]
    row = lax.broadcasted_iota(jnp.int32, (rows, DK), 0)
    col = lax.broadcasted_iota(jnp.int32, (rows, DK), 1)
    prefix_ref[0] = jnp.where(row == col, 1.0, 0.0)
    running = maps_ref[0].astype(F32)
    for place in range(1, count):
        prefix_ref[place] = running
        added = jnp.where(row >= DK, maps_ref[place].astype(F32), 0.0)
        running = dot2(split(running), maps_ref[place, :DK]) + added
    total = running.astype(BF16)
    for place in range(total_ref.shape[0]):
        total_ref[place] = total


def start_kernel(totals_ref, prefix_ref, state_ref):
    count = totals_ref.shape[0]
    place = lax.axis_index("z")
    half = totals_ref.shape[1] - DK
    state = jnp.zeros((half, DK), F32)
    for earlier in range(count - 1):
        later = totals_ref[earlier, DK:].astype(F32)
        if earlier > 0:
            later = later + dot2(split(state), totals_ref[earlier, :DK])
        state = jnp.where(earlier < place, later, state)
    parts = split(state)
    for step in range(prefix_ref.shape[0]):
        moved = prefix_ref[step, DK:] + dot3(parts, split(prefix_ref[step, :DK]))
        state_ref[step] = moved.astype(BF16)


def finish_kernel(base_ref, reach_ref, state_ref, gate_ref, gain_ref, weight_ref, out_ref):
    heads = base_ref.shape[1] // DV
    gain = gain_ref[...]
    pieces = []
    for h in range(heads):
        cols = slice(h * DV, (h + 1) * DV)
        core = base_ref[:, cols] + dot(reach_ref[:, cols], state_ref[h], NT)
        scale = lax.rsqrt(jnp.mean(core * core, axis=-1, keepdims=True) + 1e-06)
        gate = silu(gate_ref[:, cols].astype(F32))
        pieces.append((core * scale * gain * gate).astype(BF16))
    gated = jnp.concatenate(pieces, axis=1)
    width = 512
    for start in range(0, out_ref.shape[1], width):
        cols = slice(start, start + width)
        out_ref[:, cols] = dot(gated, weight_ref[:, cols]).astype(BF16)


def call(kernel, outs, *args, hbm=(), hbm_outs=False, scratch=(), limit=24, cost=None):
    vmem = pl.BlockSpec(memory_space=pltpu.VMEM)
    far = pl.BlockSpec(memory_space=pltpu.HBM)
    return pl.pallas_call(
        kernel,
        out_shape=outs,
        in_specs=[far if i in hbm else vmem for i in range(len(args))],
        out_specs=jax.tree.map(lambda _: far if hbm_outs else vmem, outs),
        scratch_shapes=list(scratch),
        cost_estimate=cost,
        compiler_params=pltpu.CompilerParams(vmem_limit_bytes=limit << 20),
        interpret=pltpu.InterpretParams() if INTERPRET else False,
    )(*args)


def local(
    nz,
    ny,
    ntp,
    query_in,
    key_in,
    value_in,
    gate_values,
    query_conv,
    key_conv,
    value_conv,
    beta_rate,
    log_decay,
    norm_gain,
    out_weight,
):
    shape = jax.ShapeDtypeStruct
    rows = query_in.shape[0]
    heads = beta_rate.shape[0]
    rim = 16
    raw = (query_in, key_in, value_in)
    tail_rows = call(
        tail_kernel,
        shape((rim, sum(a.shape[1] for a in raw)), BF16),
        *raw,
        hbm=range(3),
        scratch=(pltpu.SemaphoreType.DMA((3,)),),
        limit=60,
    )
    count = nz * ny
    rim_rows = lax.ppermute(tail_rows, ("z", "y"), [(i, i + 1) for i in range(count - 1)])

    half = DV // 2
    small = (key_conv, value_conv, beta_rate, log_decay)
    inputs = (key_in, value_in, key_conv, value_conv)
    made = (shape(key_in.shape, F32), shape(value_in.shape, F32))
    early = call(
        first_kernel,
        made,
        *inputs,
        hbm=range(len(inputs)),
        hbm_outs=True,
        scratch=(
            *(pltpu.VMEM(a.shape, a.dtype) for a in (*inputs, *made)),
            pltpu.SemaphoreType.DMA((len(inputs),)),
            pltpu.SemaphoreType.DMA((len(made),)),
        ),
        limit=60,
        cost=pl.CostEstimate(flops=10**8, bytes_accessed=3 << 20, transcendentals=1 << 20),
    )
    inputs = (rim_rows, *small, *early, key_in, value_in)
    made = (
        shape((2 * heads, DK + half, DK), BF16),
        shape((heads, rows, DK + DV), BF16),
        shape(key_in.shape, BF16),
    )
    tops = (shape((rim, key_in.shape[1]), BF16), shape((rim, value_in.shape[1]), BF16))
    maps, answer, keys = call(
        prepare_kernel,
        made,
        *inputs,
        hbm=range(len(inputs)),
        hbm_outs=True,
        scratch=(
            *(pltpu.VMEM(a.shape, a.dtype) for a in (*inputs[:-2], *tops, *made)),
            pltpu.SemaphoreType.DMA((len(inputs),)),
            pltpu.SemaphoreType.DMA((2 * heads + 1,)),
        ),
        limit=60,
    )
    base, reach = call(
        reach_kernel,
        (shape((rows, heads * DV), F32), shape((rows, heads * DK), BF16)),
        rim_rows,
        query_in,
        query_conv,
        log_decay,
        answer,
        keys,
        limit=REACH_LIMIT,
    )
    maps = lax.all_to_all(maps, "y", 0, 0, tiled=True)
    maps, base, reach = lax.optimization_barrier((maps, base, reach))
    prefix, totals = call(
        line_kernel, (shape((ny, DK + half, DK), F32), shape((nz, DK + half, DK), BF16)), maps
    )
    totals = lax.all_to_all(totals, "z", 0, 0, tiled=True)
    states = call(start_kernel, shape((ny, half, DK), BF16), totals, prefix)
    states = lax.all_to_all(states, "y", 0, 0, tiled=True)
    partial = call(
        finish_kernel,
        shape((rows, out_weight.shape[1]), BF16),
        base,
        reach,
        states.reshape(heads, DV, DK),
        gate_values,
        norm_gain.reshape(1, DV),
        out_weight,
    )
    parts = lax.all_to_all(partial.reshape(ntp, rows // ntp, -1), "tp", 0, 0, tiled=True)
    return jnp.sum(parts.astype(F32), axis=0).astype(BF16)


def build(mesh):
    nz, ny, ntp = mesh.devices.shape
    ctx = ("z", "y")
    return jax.shard_map(
        functools.partial(local, nz, ny, ntp),
        mesh=mesh,
        in_specs=(
            P(ctx, "tp"),
            P(ctx, "tp"),
            P(ctx, "tp"),
            P(ctx, "tp"),
            P(None, "tp"),
            P(None, "tp"),
            P(None, "tp"),
            P("tp", ctx),
            P("tp", ctx),
            P(),
            P("tp", None),
        ),
        out_specs=P((*ctx, "tp"), None),
        check_vma=False,
    )


def solution(mesh):
    return build(Mesh(mesh.devices.reshape(8, 8, 8), ("z", "y", "tp")))
```

```python
import functools

import jax
import jax.numpy as jnp
from jax import lax
from jax.experimental import pallas as pl
from jax.experimental.pallas import tpu as pltpu
from jax.sharding import Mesh
from jax.sharding import PartitionSpec as P

DK = 128
DV = 128
F32 = jnp.float32
BF16 = jnp.bfloat16
INTERPRET = False
REACH_LIMIT = 60

NN = (((1,), (0,)), ((), ()))
NT = (((1,), (1,)), ((), ()))
TN = (((0,), (0,)), ((), ()))


def dot(a, b, dims=NN):
    return lax.dot_general(a, b, dims, preferred_element_type=F32)


def split(x):
    high = x.astype(BF16)
    return high, (x - high.astype(F32)).astype(BF16)


def dot3(a, b, dims=NN):
    return dot(a[0], b[0], dims) + (dot(a[0], b[1], dims) + dot(a[1], b[0], dims))


def dot2(a, b, dims=NN):
    return dot(a[0], b, dims) + dot(a[1], b, dims)


def silu(x):
    return x / (1.0 + jnp.exp(-x))


def conv(rim, raw, taps):
    joined = jnp.concatenate([rim, raw], axis=0).astype(F32)
    taps = taps.astype(F32)
    rows = raw.shape[0]
    count = taps.shape[0]
    base = rim.shape[0] - (count - 1)
    running = taps[0:1] * joined[base : base + rows]
    for offset in range(1, count):
        running = running + taps[offset : offset + 1] * joined[base + offset : base + offset + rows]
    return silu(running)


def fetch(pairs, sems):
    copies = [pltpu.make_async_copy(src, dst, sems.at[i]) for i, (src, dst) in enumerate(pairs)]
    for copy in copies:
        copy.start()
    return copies


def tail_kernel(q_hbm, k_hbm, v_hbm, out_ref, sems):
    rows = q_hbm.shape[0]
    count = out_ref.shape[0]
    start = 0
    pairs = []
    for source in (q_hbm, k_hbm, v_hbm):
        width = source.shape[1]
        pairs.append((source.at[pl.ds(rows - count, count)], out_ref.at[:, pl.ds(start, width)]))
        start += width
    for copy in fetch(pairs, sems):
        copy.wait()


def wide_left(parts):
    return jnp.concatenate(parts, axis=1)


def wide_right(parts):
    high, low = parts
    top = jnp.concatenate([high, low], axis=1)
    return jnp.concatenate([top, jnp.concatenate([high, jnp.zeros_like(low)], axis=1)], axis=0)


def packed(left, right):
    both = dot(left, right)
    width = both.shape[1] // 2
    return both[:, :width] + both[:, width:]


def triangle(shape):
    row = lax.broadcasted_iota(jnp.int32, shape, 0)
    col = lax.broadcasted_iota(jnp.int32, shape, 1)
    return row, col


def pieces(value):
    high = value.astype(BF16).astype(F32)
    rest = value - high
    mid = rest.astype(BF16).astype(F32)
    return jnp.concatenate([high, mid, rest - mid], axis=0).astype(BF16)


def column_sums(left, parts):
    wide = dot(left, parts, NT)
    count = wide.shape[1] // 3
    return wide[:, :count] + (wide[:, count : 2 * count] + wide[:, 2 * count :])


def row_sums(left, parts):
    tall = dot(parts, left, NT)
    count = tall.shape[0] // 3
    return tall[:count] + (tall[count : 2 * count] + tall[2 * count :])


def clock(decay_ref, beta_ref, rows):
    row, col = triangle((rows, rows))
    ones = jnp.where(row >= col, 1.0, 0.0).astype(BF16)
    eye = jnp.where(row == col, 1.0, 0.0).astype(BF16)
    parts = pieces(jnp.concatenate([decay_ref[...], beta_ref[...]], axis=0))
    return column_sums(ones, parts), row_sums(ones, parts), column_sums(eye, parts)


def lower_block(upto_col, upto_row, plain_col, inner, h, heads, rows, cols):
    spread = upto_col[rows, h : h + 1] - upto_row[h : h + 1, cols]
    scaled = plain_col[rows, heads + h : heads + h + 1] * jnp.exp(jnp.minimum(spread, 0.0))
    return scaled * inner


def unit(rows_of_keys):
    return rows_of_keys * lax.rsqrt(jnp.sum(rows_of_keys * rows_of_keys, axis=-1, keepdims=True) + 1e-06)


def level_masks(side):
    row, col = triangle((side, side))
    size = 2
    while size < side:
        yield (row // (2 * size) == col // (2 * size)) & (row // size > col // size)
        size *= 2


def start_inverse(lower):
    row, col = triangle(lower.shape)
    return jnp.where(row == col, 1.0, 0.0) - jnp.where(row // 2 == col // 2, lower, 0.0)


def half_level(pick, lower, solved):
    off = [jnp.where(pick, part, jnp.zeros_like(part)) for part in lower]
    x = split(solved)
    return x, packed(wide_left(off), wide_right(x))


def first_kernel(
    k_hbm,
    v_hbm,
    kt_hbm,
    vt_hbm,
    keys_hbm,
    values_hbm,
    k_ref,
    v_ref,
    kt_ref,
    vt_ref,
    keys_ref,
    values_ref,
    sems,
    out_sems,
):
    copies = fetch(((kt_hbm, kt_ref), (k_hbm, k_ref), (vt_hbm, vt_ref), (v_hbm, v_ref)), sems)
    empty = jnp.zeros((16, DK), BF16)
    copies[0].wait()
    copies[1].wait()
    for start in range(0, k_ref.shape[1], DK):
        cols = slice(start, start + DK)
        keys_ref[:, cols] = unit(conv(empty, k_ref[:, cols], kt_ref[:, cols]))
    sends = [pltpu.make_async_copy(keys_ref, keys_hbm, out_sems.at[0])]
    sends[0].start()
    copies[2].wait()
    copies[3].wait()
    for start in range(0, v_ref.shape[1], DV):
        cols = slice(start, start + DV)
        values_ref[:, cols] = conv(empty, v_ref[:, cols], vt_ref[:, cols])
    sends.append(pltpu.make_async_copy(values_ref, values_hbm, out_sems.at[1]))
    sends[1].start()
    for copy in sends:
        copy.wait()


def prepare_kernel(
    rim_hbm,
    kt_hbm,
    vt_hbm,
    beta_hbm,
    decay_hbm,
    keys_hbm,
    values_hbm,
    k_hbm,
    v_hbm,
    maps_hbm,
    answer_hbm,
    keys_out_hbm,
    rim_ref,
    kt_ref,
    vt_ref,
    beta_ref,
    decay_ref,
    made_keys_ref,
    made_values_ref,
    k_ref,
    v_ref,
    maps_ref,
    answer_ref,
    keys_ref,
    sems,
    out_sems,
):
    rim = rim_ref.shape[0]
    copies = fetch(
        (
            (decay_hbm, decay_ref),
            (beta_hbm, beta_ref),
            (rim_hbm, rim_ref),
            (kt_hbm, kt_ref),
            (k_hbm.at[pl.ds(0, rim)], k_ref),
            (keys_hbm, made_keys_ref),
            (vt_hbm, vt_ref),
            (v_hbm.at[pl.ds(0, rim)], v_ref),
            (values_hbm, made_values_ref),
        ),
        sems,
    )
    sends = []

    def send(src, dst):
        copy = pltpu.make_async_copy(src, dst, out_sems.at[len(sends)])
        copy.start()
        sends.append(copy)

    rows = made_keys_ref.shape[0]
    heads = beta_ref.shape[0]
    k_cols = made_keys_ref.shape[1]
    key_heads = k_cols // DK
    ratio = heads // key_heads
    side = rows // 2
    row, col = triangle((side, side))

    copies[0].wait()
    copies[1].wait()
    upto_col, upto_row, plain_col = clock(decay_ref, beta_ref, rows)

    keys = []
    inner = []
    for copy in copies[2:6]:
        copy.wait()
    for g in range(key_heads):
        cols = slice(g * DK, (g + 1) * DK)
        top = unit(conv(rim_ref[:, k_cols + g * DK : k_cols + (g + 1) * DK], k_ref[:, cols], kt_ref[:, cols]))
        k = jnp.concatenate([top, made_keys_ref[rim:, cols]], axis=0)
        keys.append(k)
        parts = split(k)
        for i in range(2):
            keys_ref[i, :, cols] = parts[i]
        inner.append(dot3(parts, parts, NT))
    send(keys_ref, keys_out_hbm)

    spans = (slice(0, side), slice(side, rows))
    lowers = []
    solved = []
    for h in range(heads):
        part = {}
        for i, j in ((0, 0), (1, 0), (1, 1)):
            block = inner[h // ratio][spans[i], spans[j]]
            value = lower_block(upto_col, upto_row, plain_col, block, h, heads, spans[i], spans[j])
            part[i, j] = jnp.where(row > col, value, 0.0) if i == j else value
        lowers.append({key: split(value) for key, value in part.items()})
        solved.append([start_inverse(part[d, d]) for d in range(2)])

    for copy in copies[6:]:
        copy.wait()
    half = DV // 2
    lasts = [upto_col[rows - 1 : rows, h : h + 1] for h in range(heads)]
    rights = []
    tails = []

    def ready(h):
        g = h // ratio
        vcols = slice(h * DV, (h + 1) * DV)
        start = k_cols * 2 + h * DV
        top = conv(rim_ref[:, start : start + DV], v_ref[:, vcols], vt_ref[:, vcols])
        v = jnp.concatenate([top, made_values_ref[rim:, vcols]], axis=0)
        beta = plain_col[:, heads + h : heads + h + 1]
        reach = jnp.exp(upto_col[:, h : h + 1])
        rights.append(split(jnp.concatenate([(beta * reach) * keys[g], beta * v], axis=1)))
        tails.append(split(jnp.exp(lasts[h] - upto_col[:, h : h + 1]) * keys[g]))

    units = [(h, d) for h in range(heads) for d in range(2)]
    for pick in level_masks(side):
        middle = [half_level(pick, lowers[h][d, d], solved[h][d]) for h, d in units]
        if len(rights) < heads:
            ready(len(rights))
        for (h, d), (x, y) in zip(units, middle):
            solved[h][d] = solved[h][d] - packed(wide_left(x), wide_right(split(y)))
    while len(rights) < heads:
        ready(len(rights))

    done = [[split(x) for x in pair] for pair in solved]
    middle = [packed(wide_left(lowers[h][1, 0]), wide_right(done[h][0])) for h in range(heads)]
    firsts = []
    for h in range(heads):
        x0, right = done[h][0], rights[h]
        doubled = jnp.concatenate([right[0][:side]] * 2, axis=0)
        firsts.append(dot(wide_left(x0), doubled) + dot(x0[0], right[1][:side]))
    corners = [split(-packed(wide_left(done[h][1]), wide_right(split(middle[h])))) for h in range(heads)]
    answers = []
    for h in range(heads):
        bottom = [jnp.concatenate([corners[h][i], done[h][1][i]], axis=1) for i in range(2)]
        answers.append(split(jnp.concatenate([firsts[h], dot3(bottom, rights[h])], axis=0)))
        for i in range(2):
            answer_ref[h, i] = answers[h][i]
        send(answer_ref.at[h], answer_hbm.at[h])
    folds = []
    for h in range(heads):
        folded = dot(answers[h][0], jnp.concatenate(tails[h], axis=1), TN)
        folds.append(folded[:, :DK] + (folded[:, DK:] + dot(answers[h][1], tails[h][0], TN)))
    for h in range(heads):
        square = jnp.where(row[:DK, :DK] == col[:DK, :DK], jnp.exp(lasts[h]), 0.0)
        step_map = (square - folds[h][:DK]).astype(BF16)
        added = folds[h][DK:].astype(BF16)
        maps_ref[2 * h, :DK] = step_map
        maps_ref[2 * h + 1, :DK] = step_map
        maps_ref[2 * h, DK:] = added[:half]
        maps_ref[2 * h + 1, DK:] = added[half:]
        send(maps_ref.at[pl.ds(2 * h, 2)], maps_hbm.at[pl.ds(2 * h, 2)])
    for copy in sends:
        copy.wait()


def reach_kernel(rim_ref, q_ref, qt_ref, decay_ref, answer_ref, keys_ref, base_ref, reach_ref):
    rows = q_ref.shape[0]
    heads = decay_ref.shape[0]
    key_heads = q_ref.shape[1] // DK
    ratio = heads // key_heads
    side = rows // 2
    row, col = triangle((side, side))
    lower = row >= col
    wide_row, wide_col = triangle((rows, rows))
    ones = jnp.where(wide_row >= wide_col, 1.0, 0.0).astype(BF16)
    parts = pieces(jnp.concatenate([decay_ref[...], decay_ref[...]], axis=0))
    upto_col = column_sums(ones, parts)
    upto_row = row_sums(ones, parts)
    queries = []
    cross = []
    for g in range(key_heads):
        cols = slice(g * DK, (g + 1) * DK)
        q = conv(rim_ref[:, cols], q_ref[:, cols], qt_ref[:, cols])
        queries.append(q)
        cross.append(dot3(split(q), [keys_ref[i, :, cols] for i in range(2)], NT))
    spans = (slice(0, side), slice(side, rows))
    for h in range(heads):
        g = h // ratio
        vcols = slice(h * DV, (h + 1) * DV)
        sims = {}
        for i, j in ((0, 0), (1, 0), (1, 1)):
            spread = upto_col[spans[i], h : h + 1] - upto_row[h : h + 1, spans[j]]
            value = jnp.exp(jnp.minimum(spread, 0.0)) * cross[g][spans[i], spans[j]]
            sims[i, j] = split(jnp.where(lower, value, 0.0) if i == j else value)
        for i in range(2):
            left = sims[0, 0] if i == 0 else [jnp.concatenate([sims[1, 0][p], sims[1, 1][p]], axis=1) for p in range(2)]
            width = left[0].shape[1]
            emitted = dot3(left, [answer_ref[h, p, :width] for p in range(2)])
            base_ref[spans[i], vcols] = emitted[:, DK:]
            gone = jnp.exp(upto_col[spans[i], h : h + 1])
            reach_ref[spans[i], vcols] = (gone * queries[g][spans[i]] - emitted[:, :DK]).astype(BF16)


def line_kernel(maps_ref, prefix_ref, total_ref):
    count = maps_ref.shape[0]
    rows = maps_ref.shape[1]
    row = lax.broadcasted_iota(jnp.int32, (rows, DK), 0)
    col = lax.broadcasted_iota(jnp.int32, (rows, DK), 1)
    prefix_ref[0] = jnp.where(row == col, 1.0, 0.0)
    running = maps_ref[0].astype(F32)
    for place in range(1, count):
        prefix_ref[place] = running
        added = jnp.where(row >= DK, maps_ref[place].astype(F32), 0.0)
        running = dot2(split(running), maps_ref[place, :DK]) + added
    total = running.astype(BF16)
    for place in range(total_ref.shape[0]):
        total_ref[place] = total


def start_kernel(totals_ref, prefix_ref, state_ref):
    count = totals_ref.shape[0]
    place = lax.axis_index("z")
    half = totals_ref.shape[1] - DK
    state = jnp.zeros((half, DK), F32)
    for earlier in range(count - 1):
        later = totals_ref[earlier, DK:].astype(F32)
        if earlier > 0:
            later = later + dot2(split(state), totals_ref[earlier, :DK])
        state = jnp.where(earlier < place, later, state)
    parts = split(state)
    for step in range(prefix_ref.shape[0]):
        moved = prefix_ref[step, DK:] + dot3(parts, split(prefix_ref[step, :DK]))
        state_ref[step] = moved.astype(BF16)


def finish_kernel(base_ref, reach_ref, state_ref, gate_ref, gain_ref, weight_ref, out_ref):
    heads = base_ref.shape[1] // DV
    gain = gain_ref[...]
    pieces = []
    for h in range(heads):
        cols = slice(h * DV, (h + 1) * DV)
        core = base_ref[:, cols] + dot(reach_ref[:, cols], state_ref[h], NT)
        scale = lax.rsqrt(jnp.mean(core * core, axis=-1, keepdims=True) + 1e-06)
        gate = silu(gate_ref[:, cols].astype(F32))
        pieces.append((core * scale * gain * gate).astype(BF16))
    gated = jnp.concatenate(pieces, axis=1)
    width = 512
    for start in range(0, out_ref.shape[1], width):
        cols = slice(start, start + width)
        out_ref[:, cols] = dot(gated, weight_ref[:, cols]).astype(BF16)


def call(kernel, outs, *args, hbm=(), hbm_outs=False, scratch=(), limit=24, cost=None):
    vmem = pl.BlockSpec(memory_space=pltpu.VMEM)
    far = pl.BlockSpec(memory_space=pltpu.HBM)
    return pl.pallas_call(
        kernel,
        out_shape=outs,
        in_specs=[far if i in hbm else vmem for i in range(len(args))],
        out_specs=jax.tree.map(lambda _: far if hbm_outs else vmem, outs),
        scratch_shapes=list(scratch),
        cost_estimate=cost,
        compiler_params=pltpu.CompilerParams(vmem_limit_bytes=limit << 20),
        interpret=pltpu.InterpretParams() if INTERPRET else False,
    )(*args)


def local(
    nz,
    ny,
    ntp,
    query_in,
    key_in,
    value_in,
    gate_values,
    query_conv,
    key_conv,
    value_conv,
    beta_rate,
    log_decay,
    norm_gain,
    out_weight,
):
    shape = jax.ShapeDtypeStruct
    rows = query_in.shape[0]
    heads = beta_rate.shape[0]
    rim = 16
    raw = (query_in, key_in, value_in)
    tail_rows = call(
        tail_kernel,
        shape((rim, sum(a.shape[1] for a in raw)), BF16),
        *raw,
        hbm=range(3),
        scratch=(pltpu.SemaphoreType.DMA((3,)),),
        limit=60,
    )
    count = nz * ny
    rim_rows = lax.ppermute(tail_rows, ("z", "y"), [(i, i + 1) for i in range(count - 1)])

    half = DV // 2
    small = (key_conv, value_conv, beta_rate, log_decay)
    inputs = (key_in, value_in, key_conv, value_conv)
    made = (shape(key_in.shape, F32), shape(value_in.shape, F32))
    early = call(
        first_kernel,
        made,
        *inputs,
        hbm=range(len(inputs)),
        hbm_outs=True,
        scratch=(
            *(pltpu.VMEM(a.shape, a.dtype) for a in (*inputs, *made)),
            pltpu.SemaphoreType.DMA((len(inputs),)),
            pltpu.SemaphoreType.DMA((len(made),)),
        ),
        limit=60,
        cost=pl.CostEstimate(flops=10**8, bytes_accessed=3 << 20, transcendentals=1 << 20),
    )
    inputs = (rim_rows, *small, *early, key_in, value_in)
    made = (
        shape((2 * heads, DK + half, DK), BF16),
        shape((heads, 2, rows, DK + DV), BF16),
        shape((2, *key_in.shape), BF16),
    )
    tops = (shape((rim, key_in.shape[1]), BF16), shape((rim, value_in.shape[1]), BF16))
    maps, answer, keys = call(
        prepare_kernel,
        made,
        *inputs,
        hbm=range(len(inputs)),
        hbm_outs=True,
        scratch=(
            *(pltpu.VMEM(a.shape, a.dtype) for a in (*inputs[:-2], *tops, *made)),
            pltpu.SemaphoreType.DMA((len(inputs),)),
            pltpu.SemaphoreType.DMA((2 * heads + 1,)),
        ),
        limit=60,
    )
    base, reach = call(
        reach_kernel,
        (shape((rows, heads * DV), F32), shape((rows, heads * DK), BF16)),
        rim_rows,
        query_in,
        query_conv,
        log_decay,
        answer,
        keys,
        limit=REACH_LIMIT,
    )
    maps = lax.all_to_all(maps, "y", 0, 0, tiled=True)
    maps, base, reach = lax.optimization_barrier((maps, base, reach))
    prefix, totals = call(
        line_kernel, (shape((ny, DK + half, DK), F32), shape((nz, DK + half, DK), BF16)), maps
    )
    totals = lax.all_to_all(totals, "z", 0, 0, tiled=True)
    states = call(start_kernel, shape((ny, half, DK), BF16), totals, prefix)
    states = lax.all_to_all(states, "y", 0, 0, tiled=True)
    partial = call(
        finish_kernel,
        shape((rows, out_weight.shape[1]), BF16),
        base,
        reach,
        states.reshape(heads, DV, DK),
        gate_values,
        norm_gain.reshape(1, DV),
        out_weight,
    )
    parts = lax.all_to_all(partial.reshape(ntp, rows // ntp, -1), "tp", 0, 0, tiled=True)
    return jnp.sum(parts.astype(F32), axis=0).astype(BF16)


def build(mesh):
    nz, ny, ntp = mesh.devices.shape
    ctx = ("z", "y")
    return jax.shard_map(
        functools.partial(local, nz, ny, ntp),
        mesh=mesh,
        in_specs=(
            P(ctx, "tp"),
            P(ctx, "tp"),
            P(ctx, "tp"),
            P(ctx, "tp"),
            P(None, "tp"),
            P(None, "tp"),
            P(None, "tp"),
            P("tp", ctx),
            P("tp", ctx),
            P(),
            P("tp", None),
        ),
        out_specs=P((*ctx, "tp"), None),
        check_vma=False,
    )


def solution(mesh):
    return build(Mesh(mesh.devices.reshape(8, 8, 8), ("z", "y", "tp")))
```
